32 devices in a mesh: seq: 8 (over z, y), leaf: 4 (over x, core).
Axes of the slice: x: 2, y: 2, z: 4, core: 2. Of those that a mesh axis runs over, the one named last changes fastest.
Arguments:
- queries: bfloat16 [6144, 4096], P(('leaf', 'seq')), parts along dimension 0, may hold values from -6 to 6
- key_vectors: bfloat16 [6144, 4096], P(('leaf', 'seq')), parts along dimension 0, may hold values from -0.52734375 to 0.52734375
- value_vectors: bfloat16 [6144, 4096], P(('leaf', 'seq')), parts along dimension 0, may hold values from -6 to 6
- output_grad: bfloat16 [6144, 4096], P(('leaf', 'seq')), parts along dimension 0, may hold values from -6 to 6
- log_decay: float32 [6144, 32], P(('leaf', 'seq')), parts along dimension 0, may hold values from -1 to 0
- norm_gain: float32 [4096], replicated, may hold values from 0.1 to 1.9
- parent: int32 [32], P(('leaf', 'seq')), parts along dimension 0, may hold values from -1 to 6, as said below
- fork_flag: int32 [32], P(('leaf', 'seq')), parts along dimension 0, may hold values from 0 to 1, as said below
Outputs:
- attended: bfloat16 [6144, 4096], P(('leaf', 'seq')), parts along dimension 0
- query_grad: bfloat16 [6144, 4096], P(('leaf', 'seq')), parts along dimension 0
- key_grad: bfloat16 [6144, 4096], P(('leaf', 'seq')), parts along dimension 0
- value_grad: bfloat16 [6144, 4096], P(('leaf', 'seq')), parts along dimension 0
- gain_grad: float32 [16384], P('leaf'), parts along dimension 0
The draws below stay inside these ranges and needn't reach their ends.
There are 4 independent parts, one for each index of `leaf`. The reference program is written for one: setup_inputs(seed, part) draws one part's arguments, and reference() takes and returns one part's arrays. A program takes and returns all parts, laid end to end along the dimension named above; an argument that names none is the same for every part. Nothing has to cross between parts.
Inputs may be any that keep to these rules, and one draw needn't show every extreme that they name: parent[n] is -1 where block n begins a new tree (always block 0), n - 1 where it continues the block before it (always the last block), and n - 2 where it starts a new branch from the branch register. fork_flag[0] is 1 and the last block's flag is 0.
All inputs are finite; a program needn't handle non-finite values.
Results may differ from the reference program's by a relative error of at most 0.0069.
Values may be sent and summed in bfloat16 or wider, within the bound.
No kernel may reach another device: no remote copies, remote signals or barrier semaphores. Data moves between devices by JAX's collectives and lax.ppermute only.
A program may use at most 128 MiB of HBM per device.

```python
import math
import jax
import jax.numpy as jnp
from jax import lax

HEAD_COUNT = 32
DH = 128
TOK_DEV = 192
BLOCKS = 8
PACKED_TOKENS = 1536


def draw_parent(key, part):
    kind_key = jax.random.fold_in(key, 17)
    index = jnp.arange(BLOCKS, dtype=jnp.int32)
    kinds = jax.random.randint(kind_key, (BLOCKS,), 0, 8)
    root = ((kinds == 0) | (index == 0)) & (index != BLOCKS - 1)
    prev_root = jnp.concatenate([jnp.zeros((1,), jnp.bool_), root[:-1]])
    branch = (kinds >= 1) & (kinds <= 2) & ~root & ~prev_root & (index >= 2) & (index != BLOCKS - 1)
    forced = (index == 2) & ~jnp.any(branch)
    branch = branch | forced
    root = root & ~forced
    return jnp.where(root, -1, jnp.where(branch, index - 2, index - 1)).astype(jnp.int32)


def draw_fork_flag(key, part):
    fork_key = jax.random.fold_in(key, 23)
    index = jnp.arange(BLOCKS, dtype=jnp.int32)
    forks = jax.random.randint(fork_key, (BLOCKS,), 0, 2) == 1
    forks = jnp.where(index == 0, True, forks)
    forks = jnp.where(index == BLOCKS - 1, False, forks)
    return forks.astype(jnp.int32)


def draw_log_decay(key, part):
    every_key_row = jax.random.split(jax.random.fold_in(key, 29), 6)
    slow_share = 0.5
    slow = jax.random.uniform(every_key_row[0], (HEAD_COUNT,)) < slow_share
    slow_rate = -math.log(0.5) / PACKED_TOKENS
    fast_rate = jnp.exp(jax.random.uniform(every_key_row[1], (HEAD_COUNT,), jnp.float32, math.log(1.0 / 50.0), math.log(1.0 / 30.0)))
    base = jnp.where(slow, slow_rate, fast_rate)
    per_block = jnp.exp(jax.random.uniform(every_key_row[2], (BLOCKS, HEAD_COUNT), jnp.float32, math.log(0.5), math.log(2.0)))
    block_of = jnp.arange(PACKED_TOKENS, dtype=jnp.int32) // TOK_DEV
    per_token = jax.random.uniform(every_key_row[3], (PACKED_TOKENS, HEAD_COUNT), jnp.float32, 0.5, 1.5)
    event_frequency = base[None, :] * per_block[block_of] * per_token
    surge_position = jax.random.randint(every_key_row[4], (2,), 0, PACKED_TOKENS)
    surge_length = jax.random.uniform(every_key_row[5], (2, HEAD_COUNT), jnp.float32, math.log(0.5), math.log(0.8))
    match_found = jnp.arange(PACKED_TOKENS, dtype=jnp.int32)[:, None] == surge_position[None, :]
    surge_events = jnp.sum(jnp.where(match_found[:, :, None], surge_length[None, :, :], 0.0), axis=1)
    return (surge_events - event_frequency).astype(jnp.float32)


def steps_of(rng, dims, cuts, low, top_value):
    def one(position, parts):
        heights = jax.random.uniform(jax.random.fold_in(jax.random.fold_in(rng, 6), position), (parts,), jnp.float32, low / len(cuts), top_value / len(cuts))
        return jnp.repeat(jnp.exp(heights), dims[position] // parts).reshape((-1,) + (1,) * (len(dims) - position - 1))

    level = one(*cuts[0])
    for cut in cuts[1:]:
        level = level * one(*cut)
    return level


def normal_values(stream_key, extent, spread, bound, cuts=(), kind=jnp.bfloat16):
    values = jax.random.normal(stream_key, extent, jnp.float32) * spread
    if len(cuts) > 0:
        values = steps_of(stream_key, extent, cuts, -0.22, 0.18) * values
    return jnp.clip(values, min=-bound, max=bound).astype(kind)


def setup_inputs(seed: int = 0, part: int = 0) -> dict:
    keys = jax.random.split(jax.random.key(seed), 9)
    part_splits = jax.random.split(jax.random.fold_in(keys[8], part), 9)
    return {
        "queries": normal_values(part_splits[0], (PACKED_TOKENS, HEAD_COUNT * DH), 1.0, 6.0, ((0, 8),)),
        "key_vectors": normal_values(part_splits[1], (PACKED_TOKENS, HEAD_COUNT * DH), 0.0884, 0.52734375, ((0, 8),)),
        "value_vectors": normal_values(part_splits[2], (PACKED_TOKENS, HEAD_COUNT * DH), 1.0, 6.0, ((0, 8),)),
        "output_grad": normal_values(part_splits[3], (PACKED_TOKENS, HEAD_COUNT * DH), 1.0, 6.0, ((0, 8),)),
        "log_decay": draw_log_decay(jax.random.fold_in(jax.random.fold_in(keys[8], part), 71), part),
        "norm_gain": jnp.clip(1.0 + 0.18 * jax.random.normal(keys[5], (HEAD_COUNT * DH,), jnp.float32), 0.1, 1.9),
        "parent": draw_parent(jax.random.fold_in(jax.random.fold_in(keys[8], part), 71), part),
        "fork_flag": draw_fork_flag(jax.random.fold_in(jax.random.fold_in(keys[8], part), 71), part),
    }


eps = 1e-06
highest = lax.Precision.HIGHEST

def norm_heads(attention, gain):
    scale = lax.rsqrt(lax.optimization_barrier(jnp.mean(attention * attention, axis=-1, keepdims=True)) + eps)
    return attention * scale * gain

def decay_terms(log_rows):
    cum = jnp.cumsum(log_rows, axis=0)
    last = cum[-1]
    length = cum.shape[0]
    rows = lax.broadcasted_iota(jnp.int32, (length, length), 0)
    cols = lax.broadcasted_iota(jnp.int32, (length, length), 1)
    flipped = jnp.transpose(cum)
    diff = flipped[:, :, None] - flipped[:, None, :]
    mask = jnp.exp(jnp.where((rows >= cols)[None], diff, -jnp.inf))
    return (cum, last, mask)

def step_coef(alpha, beta, flag, decay):
    row_top = jnp.stack([1.0 - flag + flag * decay * beta, flag * decay * alpha], axis=-1)
    row_low = jnp.stack([decay * beta, decay * alpha], axis=-1)
    return jnp.stack([row_top, row_low], axis=1)

def kinds(parent_id, flag, index):
    alpha = (parent_id == index - 1).astype(jnp.float32)
    beta = ((parent_id >= 0) & (parent_id != index - 1)).astype(jnp.float32)
    return (alpha, beta, flag.astype(jnp.float32))

def reference(queries, key_vectors, value_vectors, output_grad, log_decay, norm_gain, parent, fork_flag):
    length = TOK_DEV
    count = BLOCKS
    gain = norm_gain.reshape(HEAD_COUNT, DH)
    shape = (count, length, HEAD_COUNT, DH)
    query_all = queries.reshape(shape)
    key_all = key_vectors.reshape(shape)
    value_all = value_vectors.reshape(shape)
    grad_all = output_grad.reshape(shape)
    decay_all = log_decay.reshape(count, length, HEAD_COUNT)
    index_all = jnp.arange(count, dtype=jnp.int32)

    def forward_block(carry, inputs):
        query_c, key_c, value_c, grad_c, log_rows, parent_id, flag, index = inputs
        cum, last, mask = decay_terms(log_rows)
        alpha, beta, flag_f = kinds(parent_id, flag, index)
        query32 = query_c.astype(jnp.float32)
        key32 = key_c.astype(jnp.float32)
        value32 = value_c.astype(jnp.float32)
        scores = jnp.einsum('ihd,jhd->hij', query32, key32, precision=highest)
        weighted = (scores * mask).astype(jnp.bfloat16)
        scaled_query = (query32 * jnp.exp(cum)[:, :, None]).astype(jnp.bfloat16)
        scaled_key = (key32 * jnp.exp(last - cum)[:, :, None]).astype(jnp.bfloat16)
        block_state = jnp.einsum('jhx,jhy->hxy', scaled_key.astype(jnp.float32), value32, precision=highest)
        block_state = lax.optimization_barrier(block_state.astype(jnp.bfloat16)).astype(jnp.float32)
        state_in = alpha * carry[1] + beta * carry[0]
        state_b = state_in.astype(jnp.bfloat16).astype(jnp.float32)
        attention = jnp.einsum('hij,jhd->ihd', weighted.astype(jnp.float32), value32, precision=highest)
        attention = attention + jnp.einsum('ihx,hxy->ihy', scaled_query.astype(jnp.float32), state_b, precision=highest)
        attended, pull = jax.vjp(norm_heads, attention, gain)
        att_grad, gain_part = pull(grad_c.astype(jnp.float32))
        att_grad_b = att_grad.astype(jnp.bfloat16)
        grad32 = att_grad_b.astype(jnp.float32)
        between = jnp.einsum('ihd,jhd->hij', grad32, value32, precision=highest)
        grad_weights = (between * mask).astype(jnp.bfloat16)
        query_grad = jnp.einsum('hij,jhd->ihd', grad_weights.astype(jnp.float32), key32, precision=highest)
        query_grad = query_grad + jnp.exp(cum)[:, :, None] * jnp.einsum('ihy,hxy->ihx', grad32, state_b, precision=highest)
        state_pull = jnp.einsum('ihx,ihy->hxy', scaled_query.astype(jnp.float32), grad32, precision=highest)
        state_pull = lax.optimization_barrier(state_pull.astype(jnp.bfloat16)).astype(jnp.float32)
        coef = step_coef(alpha, beta, flag_f, jnp.exp(last))
        moved = jnp.einsum('hab,bhxy->ahxy', coef, carry, precision=highest)
        moved = moved + jnp.stack([flag_f * block_state, block_state])
        return (moved, (attended.astype(jnp.bfloat16), query_grad.astype(jnp.bfloat16), att_grad_b, state_pull, gain_part))
    start = jnp.zeros((2, HEAD_COUNT, DH, DH), jnp.float32)
    _, (attended, query_grad, att_grads, pulls, gain_parts) = lax.scan(forward_block, start, (query_all, key_all, value_all, grad_all, decay_all, parent, fork_flag, index_all))

    def backward_block(carry, inputs):
        query_c, key_c, value_c, grad_b, log_rows, parent_id, flag, index, state_pull = inputs
        cum, last, mask = decay_terms(log_rows)
        alpha, beta, flag_f = kinds(parent_id, flag, index)
        query32 = query_c.astype(jnp.float32)
        key32 = key_c.astype(jnp.float32)
        value32 = value_c.astype(jnp.float32)
        grad32 = grad_b.astype(jnp.float32)
        scores = jnp.einsum('ihd,jhd->hij', query32, key32, precision=highest)
        weighted = (scores * mask).astype(jnp.bfloat16).astype(jnp.float32)
        between = jnp.einsum('ihd,jhd->hij', grad32, value32, precision=highest)
        grad_weights = (between * mask).astype(jnp.bfloat16).astype(jnp.float32)
        scaled_key = (key32 * jnp.exp(last - cum)[:, :, None]).astype(jnp.bfloat16).astype(jnp.float32)
        scaled_value = (value32 * jnp.exp(last - cum)[:, :, None]).astype(jnp.bfloat16).astype(jnp.float32)
        state_grad = carry[1] + flag_f * carry[0]
        grad_state_b = state_grad.astype(jnp.bfloat16).astype(jnp.float32)
        key_grad = jnp.einsum('hij,ihd->jhd', grad_weights, query32, precision=highest)
        key_grad = key_grad + jnp.einsum('jhy,hxy->jhx', scaled_value, grad_state_b, precision=highest)
        value_grad = jnp.einsum('hij,ihd->jhd', weighted, grad32, precision=highest)
        value_grad = value_grad + jnp.einsum('jhx,hxy->jhy', scaled_key, grad_state_b, precision=highest)
        back = jnp.swapaxes(step_coef(alpha, beta, flag_f, jnp.exp(last)), 1, 2)
        moved = jnp.einsum('hab,bhxy->ahxy', back, carry, precision=highest)
        moved = moved + jnp.stack([beta * state_pull, alpha * state_pull])
        return (moved, (key_grad.astype(jnp.bfloat16), value_grad.astype(jnp.bfloat16)))
    _, (key_grad, value_grad) = lax.scan(backward_block, start, (query_all, key_all, value_all, att_grads, decay_all, parent, fork_flag, index_all, pulls), reverse=True)
    flat = (PACKED_TOKENS, HEAD_COUNT * DH)
    gain_grad = lax.optimization_barrier(jnp.sum(gain_parts, axis=0)).reshape(HEAD_COUNT * DH)
    return (attended.reshape(flat), query_grad.reshape(flat), key_grad.reshape(flat), value_grad.reshape(flat), gain_grad)
```

```python
import functools
import jax
import jax.numpy as jnp
from jax import lax
from jax.experimental import pallas as pl
from jax.experimental.pallas import tpu as pltpu
from jax.sharding import PartitionSpec as P

eps = 1e-06
highest = lax.Precision.HIGHEST
f32 = jnp.float32
bf16 = jnp.bfloat16
GROUP = 4
CHUNKS = 2


def dot(a, b, ca, cb):
    return lax.dot_general(a, b, (((ca,), (cb,)), ((), ())), preferred_element_type=f32)


def split3(x):
    hi = x.astype(bf16).astype(f32)
    mid = (x - hi).astype(bf16).astype(f32)
    low = (x - hi - mid).astype(bf16).astype(f32)
    return [hi, mid, low]


def pack_rows(rows, count):
    ids = lax.broadcasted_iota(jnp.int32, (count, rows[0].shape[-1]), 0)
    out = jnp.zeros(ids.shape, f32)
    for r, row in enumerate(rows):
        out = jnp.where(ids == r, row, out)
    return out.astype(bf16)


def column(cum, head):
    ids = lax.broadcasted_iota(jnp.int32, cum.shape, 1)
    return jnp.sum(jnp.where(ids == head, cum, 0.0), axis=1, keepdims=True)


def route(step, source, targets):
    for i, target in enumerate(targets):

        @pl.when(step == i)
        def _(target=target):
            target[...] = source[...]


def fetch(step, sources, target):
    for i, source in enumerate(sources):

        @pl.when(step == i)
        def _(source=source):
            target[...] = source[...]


class Plan:
    def __init__(self, length, heads, width, devices):
        self.length, self.heads, self.width, self.devices = length, heads, width, devices
        self.per = heads // CHUNKS // GROUP
        self.rows = self.per * width
        self.extra = -(-(3 * self.per + 3) // 16) * 16
        self.piece = self.rows + self.extra
        self.cols = self.per * width
        self.chunk_cols = GROUP * self.cols

    def head(self, chunk, step, scal, t):
        return (chunk * GROUP + (step ^ scal[0])) * self.per + t

    def fixed(self, shape):
        return pl.BlockSpec(shape, lambda k, s: (0,) * len(shape))

    def real(self, chunk):
        return pl.BlockSpec((self.length, self.cols), lambda k, s: (0, chunk * GROUP + (k ^ s[0])))

    def rel(self):
        return pl.BlockSpec((self.length, self.cols), lambda k, s: (0, k))

    def pieces(self):
        return [self.fixed((self.piece, self.width))] * GROUP

    def pieces_shape(self):
        return [jax.ShapeDtypeStruct((self.piece, self.width), bf16)] * GROUP


def call(body, name, grid, scal, args, in_specs, outs, out_specs, scratch, flops, moved, aliases=None):
    return pl.pallas_call(
        body,
        name=name,
        out_shape=outs,
        grid_spec=pltpu.PrefetchScalarGridSpec(
            num_scalar_prefetch=1,
            grid=grid,
            in_specs=in_specs,
            out_specs=out_specs,
            scratch_shapes=scratch,
        ),
        input_output_aliases=aliases or {},
        cost_estimate=pl.CostEstimate(flops=flops, bytes_accessed=moved, transcendentals=0),
    )(scal, *args)


def state_body(p, chunk, first, scal, decay, keys, values, *refs):
    outs, refs = refs[:GROUP], refs[GROUP:]
    step = pl.program_id(0)
    if first:
        cum_ref, flip_ref, blk = refs

        @pl.when(step == 0)
        def _():
            rows = lax.broadcasted_iota(jnp.int32, (p.length, p.length), 0)
            cols = lax.broadcasted_iota(jnp.int32, (p.length, p.length), 1)
            tri = (rows >= cols).astype(f32)
            dims = (((1,), (0,)), ((), ()))
            cum_ref[...] = lax.dot_general(tri, decay[...], dims, precision=highest, preferred_element_type=f32)
            flip_ref[...] = jnp.transpose(cum_ref[...])

    else:
        cum_ref, blk = decay, refs[0]
    cum = cum_ref[...]
    marks = []
    for t in range(p.per):
        at = slice(t * p.width, (t + 1) * p.width)
        col = column(cum, p.head(chunk, step, scal, t))
        last = col[p.length - 1 : p.length]
        scaled = (keys[:, at].astype(f32) * jnp.exp(last - col)).astype(bf16)
        blk[at, :] = dot(scaled, values[:, at], 0, 0).astype(bf16)
        marks += split3(jnp.broadcast_to(jnp.exp(last), (1, p.width)))
    for j in (1, 2, 3):
        marks.append(jnp.full((1, p.width), scal[j].astype(f32)))
    blk[p.rows :, :] = pack_rows(marks, p.extra)
    route(step, blk, outs)


def state_call(p, chunk, scal, decay, keys, values):
    first = chunk == 0
    n = p.length
    outs, out_specs = p.pieces_shape(), p.pieces()
    if first:
        outs = outs + [jax.ShapeDtypeStruct((n, p.heads), f32), jax.ShapeDtypeStruct((p.heads, n), f32)]
        out_specs = out_specs + [p.fixed((n, p.heads)), p.fixed((p.heads, n))]
    return call(
        functools.partial(state_body, p, chunk, first), f"state{chunk}", (GROUP,), scal,
        (decay, keys, values),
        [p.fixed((n, p.heads)), p.real(chunk), p.real(chunk)],
        outs, out_specs,
        [pltpu.VMEM((p.piece, p.width), bf16)],
        2 * n * p.width * p.chunk_cols, 4 * n * p.chunk_cols + 2 * GROUP * p.piece * p.width,
    )


def mask_of(p, cum, flip, head):
    rows = lax.broadcasted_iota(jnp.int32, (p.length, p.length), 0)
    cols = lax.broadcasted_iota(jnp.int32, (p.length, p.length), 1)
    diff = column(cum[...], head) - flip[pl.ds(head, 1), :]
    return jnp.exp(jnp.where(rows >= cols, diff, -jnp.inf))


def within_body(p, chunk, scal, cum, flip, queries, keys, values, within, weights):
    step = pl.program_id(0)
    for t in range(p.per):
        at = slice(t * p.width, (t + 1) * p.width)
        mask = mask_of(p, cum, flip, p.head(chunk, step, scal, t))
        weighted = (dot(queries[:, at], keys[:, at], 1, 1) * mask).astype(bf16)
        weights[t] = weighted
        within[:, at] = dot(weighted, values[:, at], 1, 0)


def within_call(p, chunk, scal, cum, flip, queries, keys, values):
    n = p.length
    return call(
        functools.partial(within_body, p, chunk), f"within{chunk}", (GROUP,), scal,
        (cum, flip, queries, keys, values),
        [p.fixed((n, p.heads)), p.fixed((p.heads, n)), p.real(chunk), p.real(chunk), p.real(chunk)],
        [jax.ShapeDtypeStruct((n, p.chunk_cols), f32), jax.ShapeDtypeStruct((GROUP * p.per, n, n), bf16)],
        [p.rel(), pl.BlockSpec((p.per, n, n), lambda k, s: (k, 0, 0))],
        [],
        4 * n * n * p.chunk_cols, 12 * n * p.chunk_cols,
    )


def gather_pieces(scal, refs, target):
    for k, ref in enumerate(refs):
        target[k ^ scal[0]] = ref[...]


def three(ref, n, row):
    parts = ref[n, pl.ds(row, 3), :].astype(f32)
    return parts[0:1] + parts[1:2] + parts[2:3]


def load_marks(p, marks, base, n, t):
    decay = sum(marks[n, base + 3 * t + j : base + 3 * t + j + 1, :].astype(f32) for j in range(3))
    at = base + 3 * p.per
    flag, alpha, beta = (marks[n, at + j : at + j + 1, :].astype(f32) for j in range(3))
    return decay, flag, alpha, beta


def forward_scan(p, start, scr, t, emit):
    branch, state = start
    at = slice(t * p.width, (t + 1) * p.width)
    for n in range(GROUP):
        decay, flag, alpha, beta = load_marks(p, scr, p.rows, n, t)
        entering = alpha * state + beta * branch
        if emit is not None:
            emit(n, at, entering)
        state = decay * entering + scr[n, at, :].astype(f32)
        branch = flag * state + (1.0 - flag) * branch
    return branch, state


def backward_scan(p, start, scr, marks, t, emit):
    branch, state = start
    at = slice(t * p.width, (t + 1) * p.width)
    for n in reversed(range(GROUP)):
        decay, flag, alpha, beta = load_marks(p, marks, 0, n, t)
        leaving = state + flag * branch
        if emit is not None:
            emit(n, at, leaving)
        through = decay * leaving + scr[n, at, :].astype(f32)
        branch, state = (1.0 - flag) * branch + beta * through, alpha * through
    return branch, state


def zero_pair(p):
    zero = jnp.zeros((p.width, p.width), f32)
    return zero, zero


def edge_body(p, scal, p0, p1, p2, p3, edge, scr):
    gather_pieces(scal, (p0, p1, p2, p3), scr)
    for t in range(p.per):
        branch, state = forward_scan(p, zero_pair(p), scr, t, None)
        edge[0, t * p.width : (t + 1) * p.width, :] = branch.astype(bf16)
        edge[1, t * p.width : (t + 1) * p.width, :] = state.astype(bf16)


def whole(shape):
    return pl.BlockSpec(shape, lambda k, s: (0,) * len(shape))


def edge_call(p, chunk, scal, pieces):
    return call(
        functools.partial(edge_body, p), f"edge{chunk}", (1,), scal, pieces,
        p.pieces(),
        jax.ShapeDtypeStruct((2, p.rows, p.width), bf16), whole((2, p.rows, p.width)),
        [pltpu.VMEM((GROUP, p.piece, p.width), bf16)],
        40 * p.rows * p.width, 12 * p.rows * p.width,
    )


def enter_body(p, scal, p0, p1, p2, p3, coming, o0, o1, o2, o3, scr, out):
    gather_pieces(scal, (p0, p1, p2, p3), scr)
    for t in range(p.per):
        at = slice(t * p.width, (t + 1) * p.width)
        start = (coming[0, at, :].astype(f32), coming[1, at, :].astype(f32))

        def emit(n, at, value):
            out[n, at, :] = value.astype(bf16)

        forward_scan(p, start, scr, t, emit)
    for k, ref in enumerate((o0, o1, o2, o3)):
        ref[...] = out[k ^ scal[0]]


def enter_call(p, chunk, scal, pieces, coming):
    return call(
        functools.partial(enter_body, p), f"enter{chunk}", (1,), scal, (*pieces, coming),
        p.pieces() + [whole((2, p.rows, p.width))],
        [jax.ShapeDtypeStruct((p.rows, p.width), bf16)] * GROUP,
        [whole((p.rows, p.width))] * GROUP,
        [pltpu.VMEM((GROUP, p.piece, p.width), bf16), pltpu.VMEM((GROUP, p.rows, p.width), bf16)],
        60 * p.rows * p.width, 20 * p.rows * p.width,
    )


def norm_body(p, chunk, scal, *refs):
    cum, within, queries, grads, gain, s0, s1, s2, s3 = refs[:9]
    refs = refs[9 + (chunk > 0) :]
    attended, grad_b = refs[0], refs[1]
    outs, blk, state = refs[2 : 2 + GROUP], refs[2 + GROUP], refs[3 + GROUP]
    step = pl.program_id(0)
    fetch(step, (s0, s1, s2, s3), state)
    marks = []
    for t in range(p.per):
        at = slice(t * p.width, (t + 1) * p.width)
        rise = jnp.exp(column(cum[...], p.head(chunk, step, scal, t)))
        scaled = (queries[:, at].astype(f32) * rise).astype(bf16)
        attention = within[:, at] + dot(scaled, state[at, :], 1, 0)
        scale = lax.rsqrt(jnp.mean(attention * attention, axis=-1, keepdims=True) + eps)
        normed = attention * scale
        gain_row = gain[:, at]
        attended[:, at] = (normed * gain_row).astype(bf16)
        out_grad = grads[:, at].astype(f32)
        part = out_grad * gain_row
        pull = jnp.mean(part * normed, axis=-1, keepdims=True)
        grad = ((part - normed * pull) * scale).astype(bf16)
        grad_b[:, at] = grad
        blk[at, :] = dot(scaled, grad, 0, 0).astype(bf16)
        marks += split3(jnp.sum(out_grad * normed, axis=0, keepdims=True))
    blk[p.rows :, :] = pack_rows(marks, p.extra)
    route(step, blk, outs)


def norm_call(p, chunk, scal, cum, within, queries, grads, gain, states, attended):
    n = p.length
    args = (cum, within, queries, grads, gain, *states)
    specs = [p.fixed((n, p.heads)), p.rel(), p.real(chunk), p.real(chunk)]
    specs.append(pl.BlockSpec((1, p.cols), lambda k, s: (0, chunk * GROUP + (k ^ s[0]))))
    specs += [p.fixed((p.rows, p.width))] * GROUP
    aliases = None
    if chunk > 0:
        aliases = {1 + len(args): 0}
        args += (attended,)
        specs.append(pl.BlockSpec(memory_space=pl.ANY))
    full = jax.ShapeDtypeStruct((n, p.heads * p.width), bf16)
    return call(
        functools.partial(norm_body, p, chunk), f"norm{chunk}", (GROUP,), scal, args, specs,
        [full, jax.ShapeDtypeStruct((n, p.chunk_cols), bf16)] + p.pieces_shape(),
        [p.real(chunk), p.rel()] + p.pieces(),
        [pltpu.VMEM((p.piece, p.width), bf16), pltpu.VMEM((p.rows, p.width), bf16)],
        4 * n * p.width * p.chunk_cols, 12 * n * p.chunk_cols, aliases,
    )


def local_body(p, chunk, scal, *refs):
    cum, flip, queries, keys, values, grad_b, weights, s0, s1, s2, s3 = refs[:11]
    query_grad, key_local, value_local, state = refs[11 + (chunk > 0) :]
    step = pl.program_id(0)
    fetch(step, (s0, s1, s2, s3), state)
    for t in range(p.per):
        at = slice(t * p.width, (t + 1) * p.width)
        head = p.head(chunk, step, scal, t)
        mask = mask_of(p, cum, flip, head)
        grad = grad_b[:, at]
        grad_weights = (dot(grad, values[:, at], 1, 1) * mask).astype(bf16)
        rise = jnp.exp(column(cum[...], head))
        query_grad[:, at] = (
            dot(grad_weights, keys[:, at], 1, 0) + rise * dot(grad, state[at, :], 1, 1)
        ).astype(bf16)
        key_local[:, at] = dot(grad_weights, queries[:, at], 0, 0)
        value_local[:, at] = dot(weights[t], grad, 0, 0)


def local_call(p, chunk, scal, cum, flip, queries, keys, values, grad_b, weights, states, query_grad):
    n = p.length
    args = (cum, flip, queries, keys, values, grad_b, weights, *states)
    specs = [p.fixed((n, p.heads)), p.fixed((p.heads, n)), p.real(chunk), p.real(chunk), p.real(chunk)]
    specs += [p.rel(), pl.BlockSpec((p.per, n, n), lambda k, s: (k, 0, 0))]
    specs += [p.fixed((p.rows, p.width))] * GROUP
    aliases = None
    if chunk > 0:
        aliases = {1 + len(args): 0}
        args += (query_grad,)
        specs.append(pl.BlockSpec(memory_space=pl.ANY))
    return call(
        functools.partial(local_body, p, chunk), f"local{chunk}", (GROUP,), scal, args, specs,
        [jax.ShapeDtypeStruct((n, p.heads * p.width), bf16)]
        + [jax.ShapeDtypeStruct((n, p.chunk_cols), f32)] * 2,
        [p.real(chunk), p.rel(), p.rel()],
        [pltpu.VMEM((p.rows, p.width), bf16)],
        10 * n * n * p.chunk_cols, 20 * n * p.chunk_cols, aliases,
    )


def gather_marks(scal, refs, target):
    for k, ref in enumerate(refs):
        target[k ^ scal[0]] = ref[...]


def mark_specs(p):
    at = p.rows // p.extra
    return [pl.BlockSpec((p.extra, p.width), lambda k, s: (at, 0))] * GROUP


def back_edge_body(p, scal, *refs):
    pulls, marks_in, (edge, gain_sum, scr, marks) = refs[:GROUP], refs[GROUP : 2 * GROUP], refs[2 * GROUP :]
    gather_pieces(scal, pulls, scr)
    gather_marks(scal, marks_in, marks)
    for t in range(p.per):
        branch, state = backward_scan(p, zero_pair(p), scr, marks, t, None)
        edge[0, t * p.width : (t + 1) * p.width, :] = branch.astype(bf16)
        edge[1, t * p.width : (t + 1) * p.width, :] = state.astype(bf16)
    gain = jnp.zeros(gain_sum.shape, f32)
    ids = lax.broadcasted_iota(jnp.int32, gain.shape, 0)
    for t in range(p.per):
        row = 0.0
        for n in range(GROUP):
            for j in range(3):
                at = p.rows + 3 * t + j
                row = row + scr[n, at : at + 1, :].astype(f32)
        gain = jnp.where(ids == t, row, gain)
    gain_sum[...] = gain


def back_edge_call(p, chunk, scal, pulls, pieces):
    wide = -(-p.per // 8) * 8
    return call(
        functools.partial(back_edge_body, p), f"back_edge{chunk}", (1,), scal, (*pulls, *pieces),
        p.pieces() + mark_specs(p),
        [jax.ShapeDtypeStruct((2, p.rows, p.width), bf16), jax.ShapeDtypeStruct((wide, p.width), f32)],
        [whole((2, p.rows, p.width)), whole((wide, p.width))],
        [pltpu.VMEM((GROUP, p.piece, p.width), bf16), pltpu.VMEM((GROUP, p.extra, p.width), bf16)],
        40 * p.rows * p.width, 12 * p.rows * p.width,
    )


def leave_body(p, scal, *refs):
    pulls, marks_in, refs = refs[:GROUP], refs[GROUP : 2 * GROUP], refs[2 * GROUP :]
    coming, gain_mine, gain_other = refs[:3]
    outs, (scr, marks, out) = refs[3 : 3 + GROUP], refs[3 + GROUP :]
    gather_pieces(scal, pulls, scr)
    gather_marks(scal, marks_in, marks)
    for t in range(p.per):
        at = slice(t * p.width, (t + 1) * p.width)
        start = (coming[0, at, :].astype(f32), coming[1, at, :].astype(f32))

        def emit(n, at, value):
            out[n, at, :] = value.astype(bf16)

        backward_scan(p, start, scr, marks, t, emit)
    total = gain_mine[...] + gain_other[...]
    rows = []
    for t in range(p.per):
        rows += split3(total[t : t + 1])
    tail = pack_rows(rows, p.extra)
    for k, ref in enumerate(outs):
        ref[: p.rows, :] = out[k ^ scal[0]]
        ref[p.rows :, :] = tail


def leave_call(p, chunk, scal, pulls, pieces, coming, gain_mine, gain_other):
    return call(
        functools.partial(leave_body, p), f"leave{chunk}", (1,), scal,
        (*pulls, *pieces, coming, gain_mine, gain_other),
        p.pieces() + mark_specs(p) + [whole((2, p.rows, p.width))] + [whole(gain_mine.shape)] * 2,
        p.pieces_shape(), p.pieces(),
        [
            pltpu.VMEM((GROUP, p.piece, p.width), bf16),
            pltpu.VMEM((GROUP, p.extra, p.width), bf16),
            pltpu.VMEM((GROUP, p.rows, p.width), bf16),
        ],
        60 * p.rows * p.width, 20 * p.rows * p.width,
    )


def final_body(p, chunk, scal, *refs):
    cum, keys, values, key_local, value_local, s0, s1, s2, s3 = refs[:9]
    key_grad, value_grad, gain_out, state = refs[9 + 2 * (chunk > 0) :]
    step = pl.program_id(0)
    fetch(step, (s0, s1, s2, s3), state)
    gains = []
    for t in range(p.per):
        at = slice(t * p.width, (t + 1) * p.width)
        col = column(cum[...], p.head(chunk, step, scal, t))
        fall = jnp.exp(col[p.length - 1 : p.length] - col)
        scaled_key = (keys[:, at].astype(f32) * fall).astype(bf16)
        scaled_value = (values[:, at].astype(f32) * fall).astype(bf16)
        key_grad[:, at] = (key_local[:, at] + dot(scaled_value, state[at, :], 1, 1)).astype(bf16)
        value_grad[:, at] = (value_local[:, at] + dot(scaled_key, state[at, :], 1, 0)).astype(bf16)
        base = p.rows + 3 * t
        gain_out[step ^ scal[0], t : t + 1, :] = sum(
            state[base + j : base + j + 1, :].astype(f32) for j in range(3)
        )


def final_call(p, chunk, scal, cum, keys, values, key_local, value_local, states, key_grad, value_grad):
    n = p.length
    args = (cum, keys, values, key_local, value_local, *states)
    specs = [p.fixed((n, p.heads)), p.real(chunk), p.real(chunk), p.rel(), p.rel()] + p.pieces()
    aliases = None
    if chunk > 0:
        aliases = {1 + len(args): 0, 2 + len(args): 1}
        args += (key_grad, value_grad)
        specs += [pl.BlockSpec(memory_space=pl.ANY)] * 2
    full = jax.ShapeDtypeStruct((n, p.heads * p.width), bf16)
    return call(
        functools.partial(final_body, p, chunk), f"final{chunk}", (GROUP,), scal, args, specs,
        [full, full, jax.ShapeDtypeStruct((GROUP, p.per, p.width), f32)],
        [p.real(chunk), p.real(chunk), p.fixed((GROUP, p.per, p.width))],
        [pltpu.VMEM((p.piece, p.width), bf16)],
        4 * n * p.width * p.chunk_cols, 16 * n * p.chunk_cols, aliases,
    )


def exchange(p, pieces):
    out = [pieces[0]]
    for k in range(1, GROUP):
        pairs = [(i, i ^ k) for i in range(p.devices)]
        out.append(lax.ppermute(pieces[k], "seq", pairs))
    return out


def shift(p, x, groups):
    pairs = [(i, i + GROUP * groups) for i in range(p.devices) if 0 <= i + GROUP * groups < p.devices]
    return lax.ppermute(x, "seq", pairs)


def group_matrix(p, scal, pieces):
    marks = jnp.stack([piece[p.rows :, 0] for piece in pieces]).astype(f32)
    marks = marks[jnp.arange(GROUP) ^ scal[0]]
    at = 3 * p.per
    decay = marks[:, :at].reshape(GROUP, p.per, 3).sum(-1)
    flag, alpha, beta = (marks[:, at + j : at + j + 1] for j in range(3))
    top = jnp.stack([1.0 - flag + flag * decay * beta, flag * decay * alpha], axis=-1)
    low = jnp.stack([decay * beta, decay * alpha], axis=-1)
    coef = jnp.stack([top, low], axis=2)
    total = coef[0]
    for n in range(1, GROUP):
        total = jnp.einsum("hab,hbc->hac", coef[n], total, precision=highest)
    return total


def across(p, edge, matrix, sign):
    groups = p.devices // GROUP
    if groups <= 2:
        return shift(p, edge, sign)
    shape = (2, p.per, p.width, p.width)
    carry = shift(p, edge, sign).astype(f32).reshape(shape)
    moved = shift(p, matrix, sign)
    reach = 1
    while reach < groups - 1:
        carry_far = shift(p, carry, sign * reach)
        moved_far = shift(p, moved, sign * reach)
        carry = carry + jnp.einsum("hab,bhxy->ahxy", moved, carry_far, precision=highest)
        moved = jnp.einsum("hab,hbc->hac", moved, moved_far, precision=highest)
        reach *= 2
    return carry.astype(bf16).reshape(edge.shape)


def other_gain(p, gain):
    groups = p.devices // GROUP
    if groups == 2:
        return lax.ppermute(gain, "seq", [(i, i ^ GROUP) for i in range(p.devices)])
    same = [[g * GROUP + q for g in range(groups)] for q in range(GROUP)]
    return lax.psum(gain, "seq", axis_index_groups=same) - gain


def on_device(
    queries, key_vectors, value_vectors, output_grad, log_decay, norm_gain, parent, fork_flag
):
    length, heads = log_decay.shape
    width = queries.shape[1] // heads
    p = Plan(length, heads, width, lax.axis_size("seq"))
    position = lax.axis_index("seq").astype(jnp.int32)
    parent_id = parent[0]
    alpha = (parent_id == position - 1).astype(jnp.int32)
    beta = ((parent_id >= 0) & (parent_id != position - 1)).astype(jnp.int32)
    scal = jnp.stack([position % GROUP, fork_flag[0], alpha, beta])
    gain = norm_gain.reshape(1, heads * width)
    chunks = range(CHUNKS)
    many = p.devices // GROUP > 2
    pieces, withins, weights = [None] * CHUNKS, [None] * CHUNKS, [None] * CHUNKS
    cum = flip = None
    for c in chunks:
        if c == 0:
            *sent, cum, flip = state_call(p, c, scal, log_decay, key_vectors, value_vectors)
        else:
            sent = state_call(p, c, scal, cum, key_vectors, value_vectors)
        pieces[c] = exchange(p, sent)
    for c in chunks:
        withins[c], weights[c] = within_call(p, c, scal, cum, flip, queries, key_vectors, value_vectors)
    attended = query_grad = key_grad = value_grad = None
    states, pulls, locals_, matrices = [], [], [], []
    for c in chunks:
        matrices.append(group_matrix(p, scal, pieces[c]) if many else None)
        edge = edge_call(p, c, scal, pieces[c])
        coming = across(p, edge, matrices[c], 1)
        states.append(exchange(p, enter_call(p, c, scal, pieces[c], coming)))
    for c in chunks:
        attended, grad_b, *sent = norm_call(
            p, c, scal, cum, withins[c], queries, output_grad, gain, states[c], attended
        )
        pulls.append(exchange(p, sent))
        query_grad, key_local, value_local = local_call(
            p, c, scal, cum, flip, queries, key_vectors, value_vectors, grad_b, weights[c], states[c], query_grad
        )
        locals_.append((key_local, value_local))
    gains = []
    for c in chunks:
        edge, gain_mine = back_edge_call(p, c, scal, pulls[c], pieces[c])
        flipped = jnp.swapaxes(matrices[c], 1, 2) if many else None
        coming = across(p, edge, flipped, -1)
        sent = leave_call(p, c, scal, pulls[c], pieces[c], coming, gain_mine, other_gain(p, gain_mine))
        back = exchange(p, sent)
        key_grad, value_grad, gain_c = final_call(
            p, c, scal, cum, key_vectors, value_vectors, *locals_[c], back, key_grad, value_grad
        )
        gains.append(gain_c.reshape(-1))
    return attended, query_grad, key_grad, value_grad, jnp.concatenate(gains)


def solution(mesh):
    rows = P(("leaf", "seq"), None)
    flat = P(("leaf", "seq"))
    return jax.shard_map(
        on_device,
        mesh=mesh,
        in_specs=(rows, rows, rows, rows, rows, P(), flat, flat),
        out_specs=(rows, rows, rows, rows, P("leaf")),
        check_vma=False,
    )
```

```python
import functools
import jax
import jax.numpy as jnp
from jax import lax
from jax.experimental import pallas as pl
from jax.experimental.pallas import tpu as pltpu
from jax.sharding import PartitionSpec as P

eps = 1e-06
highest = lax.Precision.HIGHEST
f32 = jnp.float32
bf16 = jnp.bfloat16
GROUP = 4
CHUNKS = 2
GRANT = 24 << 20


def dot(a, b, ca, cb):
    return lax.dot_general(a, b, (((ca,), (cb,)), ((), ())), preferred_element_type=f32)


def split3(x):
    hi = x.astype(bf16).astype(f32)
    mid = (x - hi).astype(bf16).astype(f32)
    low = (x - hi - mid).astype(bf16).astype(f32)
    return [hi, mid, low]


def pack_rows(rows, count):
    ids = lax.broadcasted_iota(jnp.int32, (count, rows[0].shape[-1]), 0)
    out = jnp.zeros(ids.shape, f32)
    for r, row in enumerate(rows):
        out = jnp.where(ids == r, row, out)
    return out.astype(bf16)


def column(cum, head):
    ids = lax.broadcasted_iota(jnp.int32, cum.shape, 1)
    return jnp.sum(jnp.where(ids == head, cum, 0.0), axis=1, keepdims=True)


class Plan:
    def __init__(self, length, heads, width, devices):
        self.length, self.heads, self.width, self.devices = length, heads, width, devices
        self.chunk_heads = heads // CHUNKS
        self.per = self.chunk_heads // GROUP
        self.rows = self.per * width
        self.extra = -(-(3 * self.per + 3) // 16) * 16
        self.piece = self.rows + self.extra
        self.tail = -(-3 * self.per * CHUNKS // 16) * 16
        self.cols = self.per * width
        self.chunk_cols = GROUP * self.cols

    def at(self, q, t):
        return pl.ds(pl.multiple_of(q * self.cols + t * self.width, self.width), self.width)

    def pieces_shape(self):
        return [jax.ShapeDtypeStruct((self.piece, self.width), bf16)] * GROUP


vmem = pl.BlockSpec(memory_space=pltpu.VMEM)
smem = pl.BlockSpec(memory_space=pltpu.SMEM)
hbm = pl.BlockSpec(memory_space=pltpu.HBM)


def outside(x):
    return pltpu.with_memory_space_constraint(x, pltpu.HBM)


anywhere = pl.BlockSpec(memory_space=pl.ANY)


def call(body, args, outs, out_specs, scratch, flops, moved, specs=None, aliases=None, after=None):
    args = list(args)
    specs = list(specs or [vmem] * len(args))
    skip = 0
    if after is not None:
        args.append(after)
        specs.append(anywhere)
        skip = 1
    count = len(args)

    def kernel(*refs):
        body(*refs[: count - skip], *refs[count:])

    return pl.pallas_call(
        kernel,
        out_shape=outs,
        in_specs=specs,
        out_specs=out_specs,
        scratch_shapes=scratch,
        input_output_aliases=aliases or {},
        compiler_params=pltpu.CompilerParams(vmem_limit_bytes=GRANT),
        cost_estimate=pl.CostEstimate(flops=flops, bytes_accessed=moved, transcendentals=0),
    )(*args)


def place():
    return lax.rem(lax.axis_index("seq"), GROUP)


def route(index, source, targets):
    for i, target in enumerate(targets):

        @pl.when(index == i)
        def _(target=target):
            target[...] = source[...]


def fetch(index, sources, target):
    for i, source in enumerate(sources):

        @pl.when(index == i)
        def _(source=source):
            target[...] = source[...]


def state_body(p, chunk, parent, fork, decay, keys, values, *refs):
    first = chunk == 0
    outs, refs = refs[:GROUP], refs[GROUP:]
    scaled_key, spread, refs = refs[0], refs[1], refs[2:]
    if first:
        flip, refs = refs[0], refs[1:]
    cum, blk, key_in, value_in, sems, small_sem, decay_in = refs
    if first:
        small = pltpu.make_async_copy(decay, decay_in, small_sem)
        small.start()
    for q in range(GROUP):
        cols = slice(q * p.cols, (q + 1) * p.cols)
        far = slice(chunk * p.chunk_cols + q * p.cols, chunk * p.chunk_cols + (q + 1) * p.cols)
        for j, (src, dst) in enumerate(((keys, key_in), (values, value_in))):
            pltpu.make_async_copy(src.at[:, far], dst.at[:, cols], sems.at[j, q]).start()
    if first:
        small.wait()
        rows = lax.broadcasted_iota(jnp.int32, (p.length, p.length), 0)
        cols = lax.broadcasted_iota(jnp.int32, (p.length, p.length), 1)
        tri = (rows <= cols).astype(f32)
        dims = (((1,), (0,)), ((), ()))
        flip[...] = lax.dot_general(decay_in[...], tri, dims, precision=highest, preferred_element_type=f32)
        cum[...] = jnp.transpose(flip[...])
    else:
        cum[...] = jnp.transpose(decay[...])
    me = place()
    position = lax.axis_index("seq")
    parent_id = parent[0]
    flags = [
        fork[0],
        (parent_id == position - 1).astype(jnp.int32),
        ((parent_id >= 0) & (parent_id != position - 1)).astype(jnp.int32),
    ]

    def group(q, _):
        for j, (src, dst) in enumerate(((keys, key_in), (values, value_in))):
            cols = pl.ds(pl.multiple_of(q * p.cols, p.cols), p.cols)
            pltpu.make_async_copy(src.at[:, cols], dst.at[:, cols], sems.at[j, q]).wait()
        marks = []
        for t in range(p.per):
            at = p.at(q, t)
            col = column(cum[...], chunk * p.chunk_heads + q * p.per + t)
            last = col[p.length - 1 : p.length]
            spread[:, at] = jnp.broadcast_to(col, (p.length, p.width))
            scaled = (key_in[:, at].astype(f32) * jnp.exp(last - col)).astype(bf16)
            scaled_key[:, at] = scaled
            blk[t * p.width : (t + 1) * p.width, :] = dot(scaled, value_in[:, at], 0, 0).astype(bf16)
            marks += split3(jnp.broadcast_to(jnp.exp(last), (1, p.width)))
        for flag in flags:
            marks.append(jnp.full((1, p.width), flag.astype(f32)))
        blk[p.rows :, :] = pack_rows(marks, p.extra)
        route(q ^ me, blk, outs)
        return 0

    lax.fori_loop(0, GROUP, group, 0)


def state_call(p, chunk, parent, fork, decay, keys, values, after=None):
    n = p.length
    outs = p.pieces_shape() + [
        jax.ShapeDtypeStruct((n, p.chunk_cols), bf16),
        jax.ShapeDtypeStruct((n, p.chunk_cols), f32),
    ]
    if chunk == 0:
        outs.append(jax.ShapeDtypeStruct((p.heads, n), f32))
    return call(
        functools.partial(state_body, p, chunk),
        (parent, fork, outside(decay) if chunk == 0 else decay, outside(keys), outside(values)),
        outs, [vmem] * len(outs),
        [
            pltpu.VMEM((n, p.heads), f32),
            pltpu.VMEM((p.piece, p.width), bf16),
            pltpu.VMEM((n, p.chunk_cols), bf16),
            pltpu.VMEM((n, p.chunk_cols), bf16),
            pltpu.SemaphoreType.DMA((2, GROUP)),
            pltpu.SemaphoreType.DMA,
            pltpu.VMEM((p.heads, n), f32),
        ],
        2 * n * p.width * p.chunk_cols, 4 * n * p.chunk_cols,
        [smem, smem, hbm if chunk == 0 else vmem, hbm, hbm], after=after,
    )


def within_body(p, chunk, flip, spread, queries, keys, values, within, weights, masks, scaled_query, scaled_value):
    n, w = p.length, p.width

    def group(q, _):
        for t in range(p.per):
            at = p.at(q, t)
            far = p.at(q + chunk * GROUP, t)
            index = q * p.per + t
            cols = spread[:, at]
            row = flip[pl.ds(chunk * p.chunk_heads + index, 1), :]
            rows_id = lax.broadcasted_iota(jnp.int32, (n, n), 0)
            cols_id = lax.broadcasted_iota(jnp.int32, (n, n), 1)
            diff = jnp.concatenate([cols, cols[:, : n - w]], axis=1) - row
            mask = jnp.exp(jnp.where(rows_id >= cols_id, diff, -jnp.inf))
            masks[index] = mask
            weighted = (dot(queries[:, far], keys[:, far], 1, 1) * mask).astype(bf16)
            weights[index] = weighted
            within[:, at] = dot(weighted, values[:, far], 1, 0)
            scaled_query[:, at] = (queries[:, far].astype(f32) * jnp.exp(cols)).astype(bf16)
            fall = jnp.exp(cols[n - 1 : n] - cols)
            scaled_value[:, at] = (values[:, far].astype(f32) * fall).astype(bf16)
        return 0

    lax.fori_loop(0, GROUP, group, 0)


def within_call(p, chunk, flip, spread, queries, keys, values, after=None):
    n, h = p.length, p.chunk_heads
    outs = [
        jax.ShapeDtypeStruct((n, p.chunk_cols), f32),
        jax.ShapeDtypeStruct((h, n, n), bf16),
        jax.ShapeDtypeStruct((h, n, n), f32),
        jax.ShapeDtypeStruct((n, p.chunk_cols), bf16),
        jax.ShapeDtypeStruct((n, p.chunk_cols), bf16),
    ]
    return call(
        functools.partial(within_body, p, chunk),
        (flip, spread, queries, keys, values), outs, [vmem] * len(outs), [],
        4 * n * n * p.chunk_cols, 12 * n * p.chunk_cols, after=after,
    )


def gather_pieces(refs, target):
    me = place()
    for k, ref in enumerate(refs):
        target[k ^ me] = ref[...]


def load_marks(p, marks, base, n, t):
    decay = sum(marks[n, base + 3 * t + j : base + 3 * t + j + 1, :].astype(f32) for j in range(3))
    at = base + 3 * p.per
    flag, alpha, beta = (marks[n, at + j : at + j + 1, :].astype(f32) > 0.5 for j in range(3))
    return decay, flag, alpha, beta


def forward_scan(p, start, scr, t, emit):
    branch, state = start
    at = slice(t * p.width, (t + 1) * p.width)
    for n in range(GROUP):
        decay, flag, alpha, beta = load_marks(p, scr, p.rows, n, t)
        entering = jnp.where(alpha, state, jnp.where(beta, branch, 0.0))
        if emit is not None:
            emit(n, at, entering)
            if n == GROUP - 1:
                break
        state = decay * entering + scr[n, at, :].astype(f32)
        branch = jnp.where(flag, state, branch)
    return branch, state


def backward_scan(p, start, scr, marks, t, emit):
    branch, state = start
    at = slice(t * p.width, (t + 1) * p.width)
    for n in reversed(range(GROUP)):
        decay, flag, alpha, beta = load_marks(p, marks, 0, n, t)
        leaving = jnp.where(flag, state + branch, state)
        if emit is not None:
            emit(n, at, leaving)
            if n == 0:
                break
        through = decay * leaving + scr[n, at, :].astype(f32)
        branch = jnp.where(flag, 0.0, branch) + jnp.where(beta, through, 0.0)
        state = jnp.where(alpha, through, 0.0)
    return branch, state


def zero_pair(p):
    zero = jnp.zeros((p.width, p.width), f32)
    return zero, zero


def edge_body(p, p0, p1, p2, p3, edge, scr):
    gather_pieces((p0, p1, p2, p3), scr)
    for t in range(p.per):
        branch, state = forward_scan(p, zero_pair(p), scr, t, None)
        edge[0, t * p.width : (t + 1) * p.width, :] = branch.astype(bf16)
        edge[1, t * p.width : (t + 1) * p.width, :] = state.astype(bf16)


def edge_call(p, pieces, after=None):
    return call(
        functools.partial(edge_body, p), pieces,
        jax.ShapeDtypeStruct((2, p.rows, p.width), bf16), vmem,
        [pltpu.VMEM((GROUP, p.piece, p.width), bf16)],
        40 * p.rows * p.width, 12 * p.rows * p.width, after=after,
    )


def enter_body(p, p0, p1, p2, p3, coming, o0, o1, o2, o3, scr, out):
    gather_pieces((p0, p1, p2, p3), scr)
    for t in range(p.per):
        at = slice(t * p.width, (t + 1) * p.width)
        start = (coming[0, at, :].astype(f32), coming[1, at, :].astype(f32))

        def emit(n, at, value):
            out[n, at, :] = value.astype(bf16)

        forward_scan(p, start, scr, t, emit)
    me = place()
    for k, ref in enumerate((o0, o1, o2, o3)):
        ref[...] = out[k ^ me]


def enter_call(p, pieces, coming, after=None):
    return call(
        functools.partial(enter_body, p), (*pieces, coming),
        [jax.ShapeDtypeStruct((p.rows, p.width), bf16)] * GROUP, [vmem] * GROUP,
        [pltpu.VMEM((GROUP, p.piece, p.width), bf16), pltpu.VMEM((GROUP, p.rows, p.width), bf16)],
        60 * p.rows * p.width, 20 * p.rows * p.width, after=after,
    )


def send_out(p, chunk, q, source, target, sem):
    cols = pl.ds(pl.multiple_of(q * p.cols, p.cols), p.cols)
    far = pl.ds(pl.multiple_of(chunk * p.chunk_cols + q * p.cols, p.cols), p.cols)
    return pltpu.make_async_copy(source.at[:, cols], target.at[:, far], sem.at[q])


def norm_body(p, chunk, within, scaled_query, grads, gain, *refs):
    states, refs = refs[:GROUP], refs[GROUP + (chunk > 0) :]
    attended, grad_b = refs[0], refs[1]
    outs, (blk, state, buf, sem) = refs[2 : 2 + GROUP], refs[2 + GROUP :]
    me = place()

    def group(q, _):
        fetch(q ^ me, states, state)
        marks = []
        for t in range(p.per):
            at, far = p.at(q, t), p.at(q + chunk * GROUP, t)
            rows = slice(t * p.width, (t + 1) * p.width)
            scaled = scaled_query[:, at]
            attention = within[:, at] + dot(scaled, state[rows, :], 1, 0)
            scale = lax.rsqrt(jnp.mean(attention * attention, axis=-1, keepdims=True) + eps)
            normed = attention * scale
            gain_row = gain[:, far]
            buf[:, at] = (normed * gain_row).astype(bf16)
            lean = grads[:, far].astype(f32) * normed
            pull = jnp.mean(lean * gain_row, axis=-1, keepdims=True)
            grad = ((grads[:, far].astype(f32) * gain_row - normed * pull) * scale).astype(bf16)
            grad_b[:, at] = grad
            blk[rows, :] = dot(scaled, grad, 0, 0).astype(bf16)
            marks += split3(jnp.sum(lean, axis=0, keepdims=True))
        blk[p.rows :, :] = pack_rows(marks, p.extra)
        route(q ^ me, blk, outs)
        send_out(p, chunk, q, buf, attended, sem).start()
        return 0

    lax.fori_loop(0, GROUP, group, 0)
    for q in range(GROUP):
        send_out(p, chunk, q, buf, attended, sem).wait()


def norm_call(p, chunk, within, scaled_query, grads, gain, states, attended, after=None):
    n = p.length
    args = [within, scaled_query, grads, gain, *states]
    specs = [vmem] * len(args)
    aliases = None
    if chunk > 0:
        aliases = {len(args): 0}
        args.append(attended)
        specs.append(hbm)
    full = jax.ShapeDtypeStruct((n, p.heads * p.width), bf16)
    return call(
        functools.partial(norm_body, p, chunk), args,
        [full, jax.ShapeDtypeStruct((n, p.chunk_cols), bf16)] + p.pieces_shape(),
        [hbm, vmem] + [vmem] * GROUP,
        [
            pltpu.VMEM((p.piece, p.width), bf16),
            pltpu.VMEM((p.rows, p.width), bf16),
            pltpu.VMEM((n, p.chunk_cols), bf16),
            pltpu.SemaphoreType.DMA((GROUP,)),
        ],
        4 * n * p.width * p.chunk_cols, 12 * n * p.chunk_cols, specs, aliases, after,
    )


def local_body(p, chunk, spread, masks, queries, keys, values, grad_b, weights, *refs):
    states, refs = refs[:GROUP], refs[GROUP + (chunk > 0) :]
    query_grad, key_local, value_local, state, buf, sem = refs
    me = place()

    def group(q, _):
        fetch(q ^ me, states, state)
        for t in range(p.per):
            at, far = p.at(q, t), p.at(q + chunk * GROUP, t)
            rows = slice(t * p.width, (t + 1) * p.width)
            index = q * p.per + t
            grad = grad_b[:, at]
            grad_weights = (dot(grad, values[:, far], 1, 1) * masks[index]).astype(bf16)
            across = jnp.exp(spread[:, at]) * dot(grad, state[rows, :], 1, 1)
            buf[:, at] = (dot(grad_weights, keys[:, far], 1, 0) + across).astype(bf16)
            key_local[:, at] = dot(grad_weights, queries[:, far], 0, 0)
            value_local[:, at] = dot(weights[index], grad, 0, 0)
        send_out(p, chunk, q, buf, query_grad, sem).start()
        return 0

    lax.fori_loop(0, GROUP, group, 0)
    for q in range(GROUP):
        send_out(p, chunk, q, buf, query_grad, sem).wait()


def local_call(p, chunk, spread, masks, queries, keys, values, grad_b, weights, states, query_grad, after=None):
    n = p.length
    args = [spread, masks, queries, keys, values, grad_b, weights, *states]
    specs = [vmem] * len(args)
    aliases = None
    if chunk > 0:
        aliases = {len(args): 0}
        args.append(query_grad)
        specs.append(hbm)
    return call(
        functools.partial(local_body, p, chunk), args,
        [jax.ShapeDtypeStruct((n, p.heads * p.width), bf16)]
        + [jax.ShapeDtypeStruct((n, p.chunk_cols), f32)] * 2,
        [hbm, vmem, vmem],
        [
            pltpu.VMEM((p.rows, p.width), bf16),
            pltpu.VMEM((n, p.chunk_cols), bf16),
            pltpu.SemaphoreType.DMA((GROUP,)),
        ],
        10 * n * n * p.chunk_cols, 20 * n * p.chunk_cols, specs, aliases, after,
    )


def back_edge_body(p, chunk, *refs):
    pulls, pieces, refs = refs[:GROUP], refs[GROUP : 2 * GROUP], refs[2 * GROUP :]
    edge, gain_sum, scr, marks = refs[chunk > 0 :]
    gather_pieces(pulls, scr)
    gather_marks(p, pieces, marks)
    for t in range(p.per):
        branch, state = backward_scan(p, zero_pair(p), scr, marks, t, None)
        edge[0, t * p.width : (t + 1) * p.width, :] = branch.astype(bf16)
        edge[1, t * p.width : (t + 1) * p.width, :] = state.astype(bf16)
    gain = refs[0][...] if chunk > 0 else jnp.zeros(gain_sum.shape, f32)
    ids = lax.broadcasted_iota(jnp.int32, gain.shape, 0)
    for t in range(p.per):
        row = 0.0
        for n in range(GROUP):
            for j in range(3):
                at = p.rows + 3 * t + j
                row = row + scr[n, at : at + 1, :].astype(f32)
        gain = jnp.where(ids == chunk * p.per + t, row, gain)
    gain_sum[...] = gain


def gather_marks(p, refs, target):
    me = place()
    for k, ref in enumerate(refs):
        target[k ^ me] = ref[p.rows :, :]


def back_edge_call(p, chunk, pulls, pieces, gain_sum, after=None):
    wide = -(-p.per * CHUNKS // 8) * 8
    before = (gain_sum,) if chunk > 0 else ()
    return call(
        functools.partial(back_edge_body, p, chunk), (*pulls, *pieces, *before),
        [jax.ShapeDtypeStruct((2, p.rows, p.width), bf16), jax.ShapeDtypeStruct((wide, p.width), f32)],
        [vmem, vmem],
        [pltpu.VMEM((GROUP, p.piece, p.width), bf16), pltpu.VMEM((GROUP, p.extra, p.width), bf16)],
        40 * p.rows * p.width, 12 * p.rows * p.width, after=after,
    )


def leave_body(p, first, *refs):
    pulls, pieces, refs = refs[:GROUP], refs[GROUP : 2 * GROUP], refs[2 * GROUP :]
    coming, refs = refs[0], refs[1:]
    if first:
        gain_sum, *refs = refs
    outs, (scr, marks, out) = refs[:GROUP], refs[GROUP:]
    gather_pieces(pulls, scr)
    gather_marks(p, pieces, marks)
    for t in range(p.per):
        at = slice(t * p.width, (t + 1) * p.width)
        start = (coming[0, at, :].astype(f32), coming[1, at, :].astype(f32))

        def emit(n, at, value):
            out[n, at, :] = value.astype(bf16)

        backward_scan(p, start, scr, marks, t, emit)
    if first:
        rows = []
        for t in range(p.per * CHUNKS):
            rows += split3(gain_sum[t : t + 1, :])
        tail = pack_rows(rows, p.tail)
    me = place()
    for k, ref in enumerate(outs):
        ref[: p.rows, :] = out[k ^ me]
        if first:
            ref[p.rows :, :] = tail


def leave_call(p, chunk, pulls, pieces, coming, gains, after=None):
    first = chunk == 0
    height = p.rows + (p.tail if first else 0)
    return call(
        functools.partial(leave_body, p, first),
        (*pulls, *pieces, coming, *gains),
        [jax.ShapeDtypeStruct((height, p.width), bf16)] * GROUP, [vmem] * GROUP,
        [
            pltpu.VMEM((GROUP, p.piece, p.width), bf16),
            pltpu.VMEM((GROUP, p.extra, p.width), bf16),
            pltpu.VMEM((GROUP, p.rows, p.width), bf16),
        ],
        60 * p.rows * p.width, 20 * p.rows * p.width, after=after,
    )


def final_body(p, chunk, scaled_key, scaled_value, key_local, value_local, *refs):
    first = chunk == 0
    states, refs = refs[:GROUP], refs[GROUP:]
    if not first:
        gain_mine, gain_other, refs = refs[0], refs[1], refs[4:]
    key_grad, value_grad, gain_out, state, key_buf, value_buf, sem, *more = refs
    me = place()

    def group(q, _):
        fetch(q ^ me, states, state)
        for t in range(p.per):
            at = p.at(q, t)
            rows = slice(t * p.width, (t + 1) * p.width)
            key_buf[:, at] = (key_local[:, at] + dot(scaled_value[:, at], state[rows, :], 1, 1)).astype(bf16)
            value_buf[:, at] = (value_local[:, at] + dot(scaled_key[:, at], state[rows, :], 1, 0)).astype(bf16)
        if first:
            more[0][q] = state[p.rows :, :].astype(f32)
        send_out(p, chunk, q, key_buf, key_grad, sem.at[0]).start()
        send_out(p, chunk, q, value_buf, value_grad, sem.at[1]).start()
        return 0

    lax.fori_loop(0, GROUP, group, 0)
    if first:
        total = jnp.zeros(gain_out.shape, f32)
        ids = lax.broadcasted_iota(jnp.int32, total.shape, 0)
        for h in range(p.heads):
            c, q, t = h // p.chunk_heads, h % p.chunk_heads // p.per, h % p.per
            base = 3 * (c * p.per + t)
            row = sum(more[0][q, base + j : base + j + 1, :] for j in range(3))
            total = jnp.where(ids == h, row, total)
        gain_out[...] = total
    elif chunk == CHUNKS - 1:
        gain_out[...] = gain_mine[...] + gain_other[...]
    else:
        gain_out[...] = gain_mine[...]
    for q in range(GROUP):
        send_out(p, chunk, q, key_buf, key_grad, sem.at[0]).wait()
        send_out(p, chunk, q, value_buf, value_grad, sem.at[1]).wait()


def final_call(p, chunk, scaled_key, scaled_value, key_local, value_local, states, gains, key_grad, value_grad, after=None):
    n = p.length
    first = chunk == 0
    args = [scaled_key, scaled_value, key_local, value_local, *states]
    specs = [vmem] * len(args)
    aliases = None
    if not first:
        aliases = {len(args) + 2: 0, len(args) + 3: 1}
        args += [*gains, key_grad, value_grad]
        specs += [vmem, vmem, hbm, hbm]
    full = jax.ShapeDtypeStruct((n, p.heads * p.width), bf16)
    scratch = [
        pltpu.VMEM(states[0].shape, bf16),
        pltpu.VMEM((n, p.chunk_cols), bf16),
        pltpu.VMEM((n, p.chunk_cols), bf16),
        pltpu.SemaphoreType.DMA((2, GROUP)),
    ]
    if first:
        scratch.append(pltpu.VMEM((GROUP, p.tail, p.width), f32))
    return call(
        functools.partial(final_body, p, chunk), args,
        [full, full, jax.ShapeDtypeStruct((p.heads, p.width), f32)],
        [hbm, hbm, vmem],
        scratch,
        4 * n * p.width * p.chunk_cols, 16 * n * p.chunk_cols, specs, aliases, after,
    )


def exchange(p, pieces):
    out = [pieces[0]]
    for k in range(1, GROUP):
        pairs = [(i, i ^ k) for i in range(p.devices)]
        out.append(lax.ppermute(pieces[k], "seq", pairs))
    return out


def shift(p, x, groups):
    pairs = [(i, i + GROUP * groups) for i in range(p.devices) if 0 <= i + GROUP * groups < p.devices]
    return lax.ppermute(x, "seq", pairs)


def group_matrix(p, pieces):
    marks = jnp.stack([piece[p.rows :, 0] for piece in pieces]).astype(f32)
    marks = marks[jnp.arange(GROUP) ^ place()]
    at = 3 * p.per
    decay = marks[:, :at].reshape(GROUP, p.per, 3).sum(-1)
    flag, alpha, beta = (marks[:, at + j : at + j + 1] for j in range(3))
    top = jnp.stack([1.0 - flag + flag * decay * beta, flag * decay * alpha], axis=-1)
    low = jnp.stack([decay * beta, decay * alpha], axis=-1)
    coef = jnp.stack([top, low], axis=2)
    total = coef[0]
    for n in range(1, GROUP):
        total = jnp.einsum("hab,hbc->hac", coef[n], total, precision=highest)
    return total


def across(p, edge, matrix, sign):
    groups = p.devices // GROUP
    if groups <= 2:
        return shift(p, edge, sign)
    shape = (2, p.per, p.width, p.width)
    carry = shift(p, edge, sign).astype(f32).reshape(shape)
    moved = shift(p, matrix, sign)
    reach = 1
    while reach < groups - 1:
        carry_far = shift(p, carry, sign * reach)
        moved_far = shift(p, moved, sign * reach)
        carry = carry + jnp.einsum("hab,bhxy->ahxy", moved, carry_far, precision=highest)
        moved = jnp.einsum("hab,hbc->hac", moved, moved_far, precision=highest)
        reach *= 2
    return carry.astype(bf16).reshape(edge.shape)


def other_gain(p, gain):
    groups = p.devices // GROUP
    if groups == 2:
        return lax.ppermute(gain, "seq", [(i, i ^ GROUP) for i in range(p.devices)])
    same = [[g * GROUP + q for g in range(groups)] for q in range(GROUP)]
    return lax.psum(gain, "seq", axis_index_groups=same) - gain


ORDER = (
    "state0",
    "state1",
    "within0",
    "edge0",
    "within1",
    "edge1",
    "enter0",
    "norm0",
    "enter1",
    "back_edge0",
    "norm1",
    "local0",
    "back_edge1",
    "leave0",
    "local1",
    "final0",
    "leave1",
    "final1",
)


def on_device(
    queries, key_vectors, value_vectors, output_grad, log_decay, norm_gain, parent, fork_flag
):
    length, heads = log_decay.shape
    width = queries.shape[1] // heads
    p = Plan(length, heads, width, lax.axis_size("seq"))
    many = p.devices // GROUP > 2
    gain = norm_gain.reshape(1, heads * width)
    v = {}
    last = None

    def chained(make, pick):
        nonlocal last
        out = make(last)
        last = pick(out)
        return out

    flip = jnp.transpose(log_decay)
    attended = query_grad = key_grad = value_grad = total_gain = gain_sum = None
    for step in ORDER:
        kind, c = step[:-1], int(step[-1])
        if kind == "state":
            out = chained(
                lambda a: state_call(p, c, parent, fork_flag, flip, key_vectors, value_vectors, a),
                lambda o: o[GROUP + 1],
            )
            v["scaled_key", c], v["spread", c] = out[GROUP], out[GROUP + 1]
            if c == 0:
                flip = out[GROUP + 2]
            v["pieces", c] = exchange(p, out[:GROUP])
        elif kind == "within":
            out = chained(
                lambda a: within_call(p, c, flip, v["spread", c], queries, key_vectors, value_vectors, a),
                lambda o: o[0],
            )
            v["within", c], v["weights", c], v["masks", c], v["scaled_query", c], v["scaled_value", c] = out
        elif kind == "edge":
            pieces = v["pieces", c]
            v["matrix", c] = group_matrix(p, pieces) if many else None
            edge = chained(lambda a: edge_call(p, pieces, a), lambda o: o)
            v["coming", c] = across(p, edge, v["matrix", c], 1)
        elif kind == "enter":
            out = chained(lambda a: enter_call(p, v["pieces", c], v["coming", c], a), lambda o: o[0])
            v["states", c] = exchange(p, out)
        elif kind == "norm":
            out = chained(
                lambda a: norm_call(
                    p, c, v["within", c], v["scaled_query", c], output_grad, gain, v["states", c], attended, a
                ),
                lambda o: o[1],
            )
            attended, v["grad", c] = out[0], out[1]
            v["pulls", c] = exchange(p, out[2:])
        elif kind == "local":
            query_grad, v["key", c], v["value", c] = chained(
                lambda a: local_call(
                    p, c, v["spread", c], v["masks", c], queries, key_vectors, value_vectors,
                    v["grad", c], v["weights", c], v["states", c], query_grad, a,
                ),
                lambda o: o[1],
            )
        elif kind == "back_edge":
            edge, v["gain", c] = chained(
                lambda a: back_edge_call(p, c, v["pulls", c], v["pieces", c], gain_sum, a), lambda o: o[1]
            )
            flipped = jnp.swapaxes(v["matrix", c], 1, 2) if many else None
            v["back", c] = across(p, edge, flipped, -1)
            gain_sum = v["gain", c]
        elif kind == "leave":
            gains = (gain_sum,) if c == 0 else ()
            out = chained(
                lambda a: leave_call(p, c, v["pulls", c], v["pieces", c], v["back", c], gains, a),
                lambda o: o[0],
            )
            v["grads", c] = exchange(p, out)
        else:
            gains = (total_gain, total_gain)
            if c == CHUNKS - 1:
                gains = (total_gain, other_gain(p, total_gain))
            key_grad, value_grad, total_gain = chained(
                lambda a: final_call(
                    p, c, v["scaled_key", c], v["scaled_value", c], v["key", c], v["value", c],
                    v["grads", c], gains, key_grad, value_grad, a,
                ),
                lambda o: o[2],
            )
    return attended, query_grad, key_grad, value_grad, total_gain.reshape(-1)


def solution(mesh):
    rows = P(("leaf", "seq"), None)
    flat = P(("leaf", "seq"))
    return jax.shard_map(
        on_device,
        mesh=mesh,
        in_specs=(rows, rows, rows, rows, rows, P(), flat, flat),
        out_specs=(rows, rows, rows, rows, P("leaf")),
        check_vma=False,
    )
```
